768 devices in a mesh: row: 48 (over z_lo, x, core), col: 16 (over y, z_hi).
Axes of the slice: x: 4, y: 8, z: 12 (z_hi: 2, z_lo: 6; z = z_hi * 6 + z_lo), core: 2. Of those that a mesh axis runs over, the one named last changes fastest.
Arguments:
- harmonic: int32 [16, 1536], P('col', 'row'), may hold values from 0 to 312, as said below
- legendre: float32 [2, 16, 1536, 512], P(None, 'col', 'row'), may hold values from -6 to 6
- whitening: float32 [2, 512, 512], replicated
- longitude: float32 [2, 512], replicated, may hold values from -3.140625 to 3.140625
- observed: float32 [2, 512], replicated, may hold values from -6 to 6
Outputs:
- normal: float32 [24576, 24576], P('row', 'col')
- rhs: float32 [16, 1536], P('col', 'row')
The draws below stay inside these ranges and needn't reach their ends.
Inputs may be any that keep to these rules, and one draw needn't show every extreme that they name: `harmonic`: A value is m for a cosine column and 156 + m for a sine column (m >= 1); the columns are the first 24575 coefficients of the list ordered by degree up to 156, together with the sine coefficient of degree and order 156, each once, in a random order.
All inputs are finite; a program needn't handle non-finite values.
Results may differ from the reference program's by a relative error of at most 0.00009.
Values sent between devices are 32-bit elements; how exact they have to be, the bound alone decides.
No kernel may reach another device: no remote copies, remote signals or barrier semaphores. Data moves between devices by JAX's collectives and lax.ppermute only.
A program may use at most 32 MiB of HBM per device.

```python
import math
import jax
import jax.numpy as jnp
import numpy as np
from jax import lax

LMAX = 156
OBS = 512
ARCS = 2
COLB = 1536
P_SIZE = 24576
N_COL = 16


def draw_harmonic(key, part):
    code_list = []
    for degree in range(LMAX + 1):
        code_list.append(0)
        for order in range(1, degree + 1):
            code_list.append(order)
            code_list.append(LMAX + order)
    chosen = code_list[:P_SIZE - 1] + [2 * LMAX]
    table = jnp.asarray(np.array(chosen, dtype=np.int32))
    shuffle = jax.random.permutation(jax.random.fold_in(key, 11), P_SIZE)
    return table[shuffle].reshape(N_COL, COLB).astype(jnp.int32)


def draw_whitening(key, part):
    first_key, second_key = jax.random.split(jax.random.fold_in(key, 23), 2)
    diagonal = jax.random.uniform(first_key, (ARCS, OBS), jnp.float32, 0.5, 1.5)
    off_diag = jax.random.normal(second_key, (ARCS, OBS, OBS), jnp.float32) * (0.5 / math.sqrt(OBS))
    identity = jnp.eye(OBS, dtype=jnp.float32)
    matrix = off_diag + diagonal[:, :, None] * identity[None]
    return (matrix / math.sqrt(OBS)).astype(jnp.float32)


def steps_of(rng, dims, cuts, smallest, largest):
    def one(axis_at, blocks):
        draws = jax.random.uniform(jax.random.fold_in(jax.random.fold_in(rng, 6), axis_at), (blocks,), jnp.float32, smallest / len(cuts), largest / len(cuts))
        return jnp.repeat(jnp.exp(draws), dims[axis_at] // blocks).reshape((-1,) + (1,) * (len(dims) - axis_at - 1))

    factor_of = one(*cuts[0])
    for cut in cuts[1:]:
        factor_of = factor_of * one(*cut)
    return factor_of


def noise(rng, dims, width, most, shards=(), kind=jnp.bfloat16):
    values = jax.random.normal(rng, dims, jnp.float32) * width
    if len(shards) > 0:
        values = steps_of(rng, dims, shards, -0.22, 0.18) * values
    return jnp.clip(values, min=-most, max=most).astype(kind)


def setup_inputs(seed: int = 0) -> dict:
    streams_of = jax.random.split(jax.random.key(seed), 6)
    harmonic = draw_harmonic(jax.random.fold_in(streams_of[5], 71), 0)
    legendre = noise(streams_of[1], (ARCS, N_COL, COLB, OBS), 1.0, 6.0, ((1, 16), (2, 48)), jnp.float32)
    whitening = draw_whitening(jax.random.fold_in(streams_of[5], 71), 0)
    longitude = jnp.clip(jax.random.uniform(streams_of[3], (ARCS, OBS), jnp.float32, -3.140625, 3.140625), -3.140625, 3.140625)
    observed = noise(streams_of[4], (ARCS, OBS), 1.0, 6.0, (), jnp.float32)
    return {"harmonic": harmonic, "legendre": legendre, "whitening": whitening, "longitude": longitude, "observed": observed}


def form_columns(azimuth, leg_values, whitening, longitude):
    is_cosine = azimuth <= LMAX
    orders = jnp.where(is_cosine, azimuth, azimuth - LMAX).astype(jnp.float32)
    phase_angle = orders[None, :, None] * longitude[:, None, :]
    azimuth_terms = jnp.where(is_cosine[None, :, None], jnp.cos(phase_angle), jnp.sin(phase_angle))
    design_t = leg_values * azimuth_terms
    return jnp.einsum("apo,aqo->apq", design_t, whitening, precision=lax.Precision.HIGHEST)


def reference(harmonic, legendre, whitening, longitude, observed):
    azimuth = harmonic.reshape(-1).astype(jnp.int32)
    leg_values = legendre.reshape(ARCS, -1, OBS)
    whitened_t = form_columns(azimuth, leg_values, whitening, longitude)
    white_obs = jnp.einsum("aqo,ao->aq", whitening, observed, precision=lax.Precision.HIGHEST)
    normal = jnp.einsum("aio,ajo->ij", whitened_t, whitened_t, precision=lax.Precision.HIGHEST)
    rhs = jnp.einsum("apq,aq->p", whitened_t, white_obs, precision=lax.Precision.HIGHEST)
    return normal, rhs.reshape(N_COL, COLB)
```

```python
import jax
import jax.numpy as jnp
from jax import lax
from jax.experimental import pallas as pl
from jax.experimental.pallas import tpu as pltpu
from jax.sharding import PartitionSpec as P

LMAX = 156
ZL, XN, CN, YN, ZH = 6, 4, 2, 8, 2


def row_of(z, x, c):
    return (z * XN + x) * CN + c


def shift_row(value, dz=0, dx=0, swap=0):
    pairs = []
    for z in range(ZL):
        for x in range(XN):
            for c in range(CN):
                pairs.append((row_of((z + dz) % ZL, (x + dx) % XN, c ^ swap), row_of(z, x, c)))
    return lax.ppermute(value, "row", pairs)


def shift_col(value, dy):
    pairs = [(((y + dy) % YN) * ZH + h, y * ZH + h) for y in range(YN) for h in range(ZH)]
    return lax.ppermute(value, "col", pairs)


def scatter(value, flip):
    rows, cols = ZL * XN * CN, YN * ZH
    per = rows // cols
    pairs = []
    for big_r in range(rows):
        for big_c in range(cols):
            r = per * big_c + big_r // cols
            k = (big_r % cols) ^ flip
            pairs.append((big_r * cols + big_c, r * cols + k))
    return lax.ppermute(value, ("row", "col"), pairs)


def split(value):
    high = value.astype(jnp.bfloat16)
    low = (value - high.astype(jnp.float32)).astype(jnp.bfloat16)
    return high, low


def dot_t(a, b):
    return lax.dot_general(a, b, (((1,), (1,)), ((), ())), preferred_element_type=jnp.float32)


ROW_PARTS = ((0,), (-1,), (1,), (4,), (-2, -3), (2, 3))


def product_kernel(ids, *refs):
    row_refs = refs[: len(ROW_PARTS)]
    col_refs = refs[len(ROW_PARTS) : len(ROW_PARTS) + 2 * XN]
    out_ref, high, low, col = refs[len(ROW_PARTS) + 2 * XN :]
    my_z, my_x, my_c, my_y = ids[0], ids[1], ids[2], ids[3]
    step = pl.program_id(0)

    @pl.when(step == 0)
    def _():
        for ref, parts in zip(row_refs, ROW_PARTS):
            for at, dy in enumerate(parts):
                h, l = split(ref[at * 64 : at * 64 + 64, :])
                to = pl.multiple_of(lax.rem(my_y + dy + YN, YN) * 64, 64)
                high[pl.ds(to, 64), :] = h
                low[pl.ds(to, 64), :] = l

    dz = lax.rem(step - my_z + ZL, ZL)
    frm = pl.multiple_of(dz * 32, 32)
    for dx in range(XN):
        for s in range(CN):
            x = lax.rem(my_x + dx, XN)
            c = my_c + s - 2 * my_c * s
            to = pl.multiple_of((x * CN + c) * 32, 32)
            col[pl.ds(to, 32), :] = col_refs[s * XN + dx][pl.ds(frm, 32), :]
    ch, cl = split(col[...])
    rh, rl = high[...], low[...]
    out_ref[...] = dot_t(rh, ch) + (dot_t(rh, cl) + dot_t(rl, ch))


def product(ids, rows, cols):
    whole = pl.BlockSpec(memory_space=pltpu.VMEM)
    return pl.pallas_call(
        product_kernel,
        out_shape=jax.ShapeDtypeStruct((512, 1536), jnp.float32),
        grid_spec=pltpu.PrefetchScalarGridSpec(
            num_scalar_prefetch=1,
            grid=(ZL,),
            in_specs=[whole] * (len(rows) + len(cols)),
            out_specs=pl.BlockSpec((512, 256), lambda i, ids: (0, i)),
            scratch_shapes=[
                pltpu.VMEM((512, 1024), jnp.bfloat16),
                pltpu.VMEM((512, 1024), jnp.bfloat16),
                pltpu.VMEM((256, 1024), jnp.float32),
            ],
        ),
        compiler_params=pltpu.CompilerParams(vmem_limit_bytes=28 * 2**20),
    )(ids, *rows, *cols)


def form_columns(azimuth, leg_values, whitening, longitude):
    is_cosine = azimuth <= LMAX
    orders = jnp.where(is_cosine, azimuth, azimuth - LMAX).astype(jnp.float32)
    phase_angle = orders[None, :, None] * longitude[:, None, :]
    azimuth_terms = jnp.where(is_cosine[None, :, None], jnp.cos(phase_angle), jnp.sin(phase_angle))
    design_t = leg_values * azimuth_terms
    return [
        lax.dot_general(design_t[a], whitening[a], (((1,), (1,)), ((), ())), precision=lax.Precision.HIGHEST)
        for a in range(2)
    ]


def body(harmonic, legendre, whitening, longitude, observed):
    arcs = legendre.shape[0]
    azimuth = harmonic.reshape(-1)
    leg_values = legendre.reshape(arcs, -1, legendre.shape[3])
    own = jnp.concatenate(form_columns(azimuth, leg_values, whitening, longitude), axis=1)
    white_obs = jnp.einsum("aqo,ao->aq", whitening, observed, precision=lax.Precision.HIGHEST)
    rhs_part = jnp.einsum("pk,k->p", own, white_obs.reshape(-1), precision=lax.Precision.HIGHEST).reshape(1, -1)

    row, col = lax.axis_index("row"), lax.axis_index("col")
    ids = jnp.stack([row // (XN * CN), (row // CN) % XN, row % CN, col // ZH]).astype(jnp.int32)
    odd = (col % ZH) == 1

    first, second = scatter(own, 0), scatter(own, 1)
    by_z = [own] + [shift_row(own, dz=d) for d in range(1, ZL)]
    pair = jnp.where(odd, jnp.concatenate([second, first]), jnp.concatenate([first, second]))
    below, above = shift_col(pair, -1), shift_col(pair, 1)
    far = shift_col(pair, 4)
    below2 = shift_col(jnp.concatenate([pair, below]), -2)
    above2 = shift_col(jnp.concatenate([pair, above]), 2)

    line = jnp.concatenate(by_z)
    mine = [line] + [shift_row(line, dx=d) for d in range(1, XN)]
    theirs = [shift_row(v, swap=1) for v in mine]
    tile_sum = product(ids, [pair, below, above, far, below2, above2], mine + theirs)
    return (tile_sum, rhs_part)


def solution(mesh):
    in_specs = (P("col", "row"), P(None, "col", "row", None), P(), P(), P())
    out_specs = (P("row", "col"), P("col", "row"))
    return jax.shard_map(body, mesh=mesh, in_specs=in_specs, out_specs=out_specs, check_vma=False)
```

```python
import jax
import jax.numpy as jnp
from jax import lax
from jax.experimental import pallas as pl
from jax.experimental.pallas import tpu as pltpu
from jax.sharding import PartitionSpec as P


LMAX = 156
ZL, XN, CN, YN, ZH = 6, 4, 2, 8, 2
WIDTH = 32
TRIPLE = ZL // 2


def from_row(value, source):
    place = lambda z, x, c: (z * XN + x) * CN + c
    every = [(z, x, c) for z in range(ZL) for x in range(XN) for c in range(CN)]
    return lax.ppermute(value, "row", [(place(*source(*at)), place(*at)) for at in every])


def from_col(value, source):
    every = [(y, h) for y in range(YN) for h in range(ZH)]
    place = lambda y, h: y * ZH + h
    return lax.ppermute(value, "col", [(place(*source(*at)), place(*at)) for at in every])


def from_y(value, dy, other):
    rows, cols = ZL * XN * CN, YN * ZH
    pairs = [
        (r * cols + (y + (dy, other)[r % CN]) % YN * ZH + h, r * cols + y * ZH + h)
        for r in range(rows)
        for y in range(YN)
        for h in range(ZH)
    ]
    return lax.ppermute(value, ("row", "col"), pairs)


def scatter(value):
    rows, cols = ZL * XN * CN, YN * ZH
    pairs = [
        (big_r * cols + big_c, (rows // cols * big_c + big_r // cols) * cols + big_r % cols)
        for big_r in range(rows)
        for big_c in range(cols)
    ]
    return lax.ppermute(value, ("row", "col"), pairs)


def in_triple(z, d):
    return z // TRIPLE * TRIPLE + (z % TRIPLE + d) % TRIPLE


def split(value):
    high = value.astype(jnp.bfloat16)
    low = (value - high.astype(jnp.float32)).astype(jnp.bfloat16)
    return high, low


def dot_t(a, b):
    return lax.dot_general(a, b, (((1,), (1,)), ((), ())), preferred_element_type=jnp.float32)


def to_column(value):
    n = value.shape[1]
    same = lax.broadcasted_iota(jnp.int32, (n, n), 0) == lax.broadcasted_iota(jnp.int32, (n, n), 1)
    return jnp.sum(jnp.where(same, jnp.broadcast_to(value, (n, n)), 0.0), axis=1, keepdims=True)


def to_row(value):
    n = value.shape[0]
    same = lax.broadcasted_iota(jnp.int32, (n, n), 0) == lax.broadcasted_iota(jnp.int32, (n, n), 1)
    return jnp.sum(jnp.where(same, jnp.broadcast_to(value, (n, n)), 0.0), axis=0, keepdims=True)


def trig(angle, is_cosine):
    turns = jnp.floor(angle * 0.6366197723675814 + 0.5)
    rest = angle - turns * 1.5703125
    rest = rest - turns * 4.837512969970703125e-4
    rest = rest - turns * 7.54978995489188216e-8
    quadrant = (turns.astype(jnp.int32) + jnp.where(is_cosine, 0, 3)) & 3
    sq = rest * rest
    sine = ((-1.9515295891e-4 * sq + 8.3321608736e-3) * sq - 1.6666654611e-1) * sq * rest + rest
    cosine = ((2.443315711809948e-5 * sq - 1.388731625493765e-3) * sq + 4.166664568298827e-2) * sq * sq
    cosine = cosine - 0.5 * sq + 1.0
    value = jnp.where((quadrant & 1) == 0, cosine, sine)
    return jnp.where((quadrant == 1) | (quadrant == 2), -value, value)


def whiten_kernel(*refs):
    sources, (own_ref, rhs_ref), buffers, sems = refs[:5], refs[5:7], refs[7:12], refs[12]
    harmonic, legendre, whitening, longitude, observed = buffers
    arcs = longitude.shape[0]
    copies = [pltpu.make_async_copy(sources[i], buffers[i], sems.at[i]) for i in (0, 3, 4, 1)]
    parts = [
        pltpu.make_async_copy(sources[2].at[a], whitening.at[a], sems.at[5 + a]) for a in range(arcs)
    ]
    for copy in copies + parts:
        copy.start()
    for copy in copies:
        copy.wait()
    azimuth = to_column(harmonic[...].astype(jnp.float32))
    is_cosine = azimuth <= float(LMAX)
    order = jnp.where(is_cosine, azimuth, azimuth - float(LMAX))
    total = None
    for arc in range(arcs):
        terms = trig(order * longitude[arc : arc + 1, :], is_cosine)
        design = legendre[arc, 0] * terms
        seen = jnp.broadcast_to(observed[arc : arc + 1, :], (8, observed.shape[1]))
        dh, dl = split(jnp.concatenate([design, seen], axis=0))
        parts[arc].wait()
        wh, wl = split(whitening[arc])
        n = dh.shape[0]
        both = dot_t(jnp.concatenate([dh, dl], axis=0), wh)
        out = both[:n] + both[n:] + dot_t(dh, wl)
        own = out[:WIDTH]
        own_ref[:, arc * own.shape[1] : (arc + 1) * own.shape[1]] = own
        part = jnp.sum(own * out[WIDTH : WIDTH + 1], axis=1, keepdims=True)
        total = part if total is None else total + part
    rhs_ref[...] = to_row(total)


def whiten(*args):
    arcs, obs = args[3].shape
    return pl.pallas_call(
        whiten_kernel,
        out_shape=(
            jax.ShapeDtypeStruct((WIDTH, arcs * obs), jnp.float32),
            jax.ShapeDtypeStruct((1, WIDTH), jnp.float32),
        ),
        in_specs=[pl.BlockSpec(memory_space=pl.ANY)] * len(args),
        out_specs=(pl.BlockSpec(memory_space=pltpu.VMEM),) * 2,
        scratch_shapes=[pltpu.VMEM(v.shape, v.dtype) for v in args]
        + [pltpu.SemaphoreType.DMA((5 + arcs,))],
        compiler_params=pltpu.CompilerParams(vmem_limit_bytes=16 * 2**20),
    )(*[pltpu.with_memory_space_constraint(v, pltpu.HBM) for v in args])


ROW_PARTS = ((0,), (4,), (2, 6), (1, 5, 3, 7))
COL_PARTS = (((0, 0), (0, 1)), ((1, 0), (1, 1)), ((2, 0),), ((-1, 1), (-1, 0)), ((2, 1),))


def join_kernel(*refs):
    at = 0
    for ref in refs[:-1]:
        refs[-1][at : at + ref.shape[0], :] = ref[...]
        at += ref.shape[0]


def pair_kernel(block, twin, out):
    n = block.shape[0]
    mine = lax.rem(lax.axis_index("col"), ZH)
    out[pl.ds(pl.multiple_of(mine * n, n), n), :] = block[...]
    out[pl.ds(pl.multiple_of((1 - mine) * n, n), n), :] = twin[...]


def head_kernel(whole, out):
    out[...] = whole[: out.shape[0], :]


def local(kernel, length, *parts):
    on_core = pl.BlockSpec(memory_space=pltpu.VMEM)
    return pl.pallas_call(
        kernel,
        out_shape=jax.ShapeDtypeStruct((length, parts[0].shape[1]), parts[0].dtype),
        in_specs=[on_core] * len(parts),
        out_specs=on_core,
        compiler_params=pltpu.CompilerParams(vmem_limit_bytes=16 * 2**20),
    )(*parts)


def join(*parts):
    return local(join_kernel, sum(v.shape[0] for v in parts), *parts)


def product_kernel(*refs):
    n_row, n_col = len(ROW_PARTS), len(COL_PARTS)
    row_refs, col_refs = refs[:n_row], refs[n_row : n_row + n_col]
    out_ref, rows, *tiles = refs[n_row + n_col :]
    row, my_y = lax.axis_index("row"), lax.axis_index("col") // ZH
    my_z, my_x, my_c = row // (XN * CN), lax.rem(row // CN, XN), lax.rem(row, CN)
    sign = 1 - 2 * my_c
    at_step = pl.program_id(0)
    block = 2 * WIDTH
    tall = block * YN
    wide = XN * CN * WIDTH

    def fill(to, z):
        mirrored = (z // TRIPLE != my_z // TRIPLE).astype(jnp.int32)
        near = z + mirrored * (ZL - 1 - 2 * z)
        ahead = lax.rem(lax.rem(near, TRIPLE) - lax.rem(my_z, TRIPLE) + TRIPLE, TRIPLE)
        frm = (2 * ahead + mirrored) * WIDTH
        for ref, parts in zip(col_refs, COL_PARTS):
            for at, (dx, s) in enumerate(parts):
                x = lax.rem(my_x + sign * dx + XN, XN)
                c = my_c + s - 2 * my_c * s
                put = pl.multiple_of((x * CN + c) * WIDTH, WIDTH)
                start = pl.multiple_of(at * ZL * WIDTH + frm, WIDTH)
                h, l = split(ref[pl.ds(start, WIDTH), :])
                to[0][pl.ds(put, WIDTH), :] = h
                to[1][pl.ds(put, WIDTH), :] = l

    def multiply(tile):
        both = dot_t(rows[...], tile[0][...])
        return both[:tall] + (both[tall:] + dot_t(rows[:tall], tile[1][...]))

    @pl.when(at_step == 0)
    def _():
        for ref, parts in zip(row_refs, ROW_PARTS):
            for at, dy in enumerate(parts):
                h, l = split(ref[at * block : (at + 1) * block, :])
                to = pl.multiple_of(lax.rem(my_y + sign * dy + YN, YN) * block, block)
                rows[pl.ds(to, block), :] = h
                rows[pl.ds(tall + to, block), :] = l
        fill(tiles[:2], 0 * at_step)

    out_ref[:, :wide] = multiply(tiles[:2])
    fill(tiles[2:], 2 * at_step + 1)
    out_ref[:, wide:] = multiply(tiles[2:])
    fill(tiles[:2], jnp.minimum(2 * at_step + 2, ZL - 1))


def product(rows, cols):
    whole = pl.BlockSpec(memory_space=pltpu.VMEM)
    tall, deep = 2 * WIDTH * YN, rows[0].shape[1]
    wide = XN * CN * WIDTH
    return pl.pallas_call(
        product_kernel,
        out_shape=jax.ShapeDtypeStruct((tall, ZL * wide), jnp.float32),
        grid=(ZL // 2,),
        in_specs=[whole] * (len(rows) + len(cols)),
        out_specs=pl.BlockSpec((tall, 2 * wide), lambda i: (0, i)),
        scratch_shapes=[pltpu.VMEM((2 * tall, deep), jnp.bfloat16)]
        + [pltpu.VMEM((wide, deep), jnp.bfloat16)] * 4,
        compiler_params=pltpu.CompilerParams(vmem_limit_bytes=28 * 2**20),
    )(*rows, *cols)


def step(harmonic, legendre, whitening, longitude, observed):
    own, rhs_part = whiten(harmonic, legendre, whitening, longitude, observed)

    swap = lambda z, x, c: (z, x, 1 - c)
    block = scatter(own)
    mirror = from_row(own, lambda z, x, c: (ZL - 1 - z, x, c))
    twin = from_col(block, lambda y, h: (y, 1 - h))
    pair = local(pair_kernel, 2 * WIDTH, block, twin)

    two = join(own, mirror)
    near = [from_row(two, lambda z, x, c, d=d: (in_triple(z, d), x, c)) for d in (1, 2)]
    line = join(two, *near)

    y4 = from_y(pair, 4, 4)
    quad = join(pair, y4)
    y2 = from_y(quad, 2, -2)
    y1 = from_y(join(quad, y2), 1, -1)

    ahead = lambda z, x, c: (z, (x + 1 - 2 * c) % XN, c)
    chip = join(line, from_row(line, swap))
    x1 = from_row(chip, ahead)
    x2 = from_row(local(head_kernel, line.shape[0], x1), ahead)
    back = [from_row(v, swap) for v in (x1, x2)]
    return product([pair, y4, y2, y1], [chip, x1, x2] + back), rhs_part


def solution(mesh):
    in_specs = (P("col", "row"), P(None, "col", "row", None), P(), P(), P())
    out_specs = (P("row", "col"), P("col", "row"))
    return jax.shard_map(step, mesh=mesh, in_specs=in_specs, out_specs=out_specs, check_vma=False)
```

```python
import jax
import jax.numpy as jnp
from jax import lax
from jax.experimental import pallas as pl
from jax.experimental.pallas import tpu as pltpu
from jax.sharding import PartitionSpec as P


LMAX = 156
ZL, XN, CN, YN, ZH = 6, 4, 2, 8, 2
WIDTH = 32
TRIPLE = ZL // 2


def from_row(value, source):
    place = lambda z, x, c: (z * XN + x) * CN + c
    every = [(z, x, c) for z in range(ZL) for x in range(XN) for c in range(CN)]
    return lax.ppermute(value, "row", [(place(*source(*at)), place(*at)) for at in every])


def from_y(value, dy, other):
    rows, cols = ZL * XN * CN, YN * ZH
    pairs = [
        (r * cols + (y + (dy, other)[r % CN]) % YN * ZH + h, r * cols + y * ZH + h)
        for r in range(rows)
        for y in range(YN)
        for h in range(ZH)
    ]
    return lax.ppermute(value, ("row", "col"), pairs)


def scatter(value, flip):
    rows, cols = ZL * XN * CN, YN * ZH
    pairs = [
        (big_r * cols + big_c, (rows // cols * big_c + big_r // cols) * cols + (big_r % cols ^ flip))
        for big_r in range(rows)
        for big_c in range(cols)
    ]
    return lax.ppermute(value, ("row", "col"), pairs)


def in_triple(z, d):
    return z // TRIPLE * TRIPLE + (z % TRIPLE + d) % TRIPLE


def split(value):
    high = value.astype(jnp.bfloat16)
    low = (value - high.astype(jnp.float32)).astype(jnp.bfloat16)
    return high, low


def dot_t(a, b):
    return lax.dot_general(a, b, (((1,), (1,)), ((), ())), preferred_element_type=jnp.float32)


def to_column(value):
    n = value.shape[1]
    same = lax.broadcasted_iota(jnp.int32, (n, n), 0) == lax.broadcasted_iota(jnp.int32, (n, n), 1)
    return jnp.sum(jnp.where(same, jnp.broadcast_to(value, (n, n)), 0.0), axis=1, keepdims=True)


def to_row(value):
    n = value.shape[0]
    same = lax.broadcasted_iota(jnp.int32, (n, n), 0) == lax.broadcasted_iota(jnp.int32, (n, n), 1)
    return jnp.sum(jnp.where(same, jnp.broadcast_to(value, (n, n)), 0.0), axis=0, keepdims=True)


def trig(angle, is_cosine):
    turns = jnp.floor(angle * 0.6366197723675814 + 0.5)
    rest = angle - turns * 1.5703125
    rest = rest - turns * 4.837512969970703125e-4
    rest = rest - turns * 7.54978995489188216e-8
    quadrant = (turns.astype(jnp.int32) + jnp.where(is_cosine, 0, 3)) & 3
    sq = rest * rest
    sine = ((-1.9515295891e-4 * sq + 8.3321608736e-3) * sq - 1.6666654611e-1) * sq * rest + rest
    cosine = ((2.443315711809948e-5 * sq - 1.388731625493765e-3) * sq + 4.166664568298827e-2) * sq * sq
    cosine = cosine - 0.5 * sq + 1.0
    value = jnp.where((quadrant & 1) == 0, cosine, sine)
    return jnp.where((quadrant == 1) | (quadrant == 2), -value, value)


def whiten_kernel(*refs):
    sources, (own_ref, rhs_ref), buffers, sems = refs[:5], refs[5:7], refs[7:12], refs[12]
    harmonic, legendre, whitening, longitude, observed = buffers
    arcs = longitude.shape[0]
    copies = [pltpu.make_async_copy(sources[i], buffers[i], sems.at[i]) for i in (0, 3, 4, 1)]
    parts = [
        pltpu.make_async_copy(sources[2].at[a], whitening.at[a], sems.at[5 + a]) for a in range(arcs)
    ]
    for copy in copies + parts:
        copy.start()
    for copy in copies:
        copy.wait()
    azimuth = to_column(harmonic[...].astype(jnp.float32))
    is_cosine = azimuth <= float(LMAX)
    order = jnp.where(is_cosine, azimuth, azimuth - float(LMAX))
    total = None
    for arc in range(arcs):
        terms = trig(order * longitude[arc : arc + 1, :], is_cosine)
        design = legendre[arc, 0] * terms
        seen = jnp.broadcast_to(observed[arc : arc + 1, :], (8, observed.shape[1]))
        dh, dl = split(jnp.concatenate([design, seen], axis=0))
        parts[arc].wait()
        wh, wl = split(whitening[arc])
        n = dh.shape[0]
        both = dot_t(jnp.concatenate([dh, dl], axis=0), wh)
        out = both[:n] + both[n:] + dot_t(dh, wl)
        own = out[:WIDTH]
        own_ref[:, arc * own.shape[1] : (arc + 1) * own.shape[1]] = own
        part = jnp.sum(own * out[WIDTH : WIDTH + 1], axis=1, keepdims=True)
        total = part if total is None else total + part
    rhs_ref[...] = to_row(total)


def whiten(*args):
    arcs, obs = args[3].shape
    return pl.pallas_call(
        whiten_kernel,
        out_shape=(
            jax.ShapeDtypeStruct((WIDTH, arcs * obs), jnp.float32),
            jax.ShapeDtypeStruct((1, WIDTH), jnp.float32),
        ),
        in_specs=[pl.BlockSpec(memory_space=pl.ANY)] * len(args),
        out_specs=(pl.BlockSpec(memory_space=pltpu.VMEM),) * 2,
        scratch_shapes=[pltpu.VMEM(v.shape, v.dtype) for v in args]
        + [pltpu.SemaphoreType.DMA((5 + arcs,))],
        compiler_params=pltpu.CompilerParams(vmem_limit_bytes=16 * 2**20),
    )(*[pltpu.with_memory_space_constraint(v, pltpu.HBM) for v in args])


ROW_PARTS = ((0,), (4,), (2, 6), (1, 5, 3, 7))
COL_PARTS = (((0, 0),), ((0, 1),), ((1, 0),), ((1, 1),), ((2, 0),), ((-1, 1),), ((-1, 0),), ((2, 1),))


def join_kernel(*refs):
    at = 0
    for ref in refs[:-1]:
        refs[-1][at : at + ref.shape[0], :] = ref[...]
        at += ref.shape[0]


def pair_kernel(block, twin, out):
    n = block.shape[0]
    mine = lax.rem(lax.axis_index("col"), ZH)
    out[pl.ds(pl.multiple_of(mine * n, n), n), :] = block[...]
    out[pl.ds(pl.multiple_of((1 - mine) * n, n), n), :] = twin[...]


def local(kernel, length, *parts):
    on_core = pl.BlockSpec(memory_space=pltpu.VMEM)
    return pl.pallas_call(
        kernel,
        out_shape=jax.ShapeDtypeStruct((length, parts[0].shape[1]), parts[0].dtype),
        in_specs=[on_core] * len(parts),
        out_specs=on_core,
        compiler_params=pltpu.CompilerParams(vmem_limit_bytes=16 * 2**20),
    )(*parts)


def join(*parts):
    return local(join_kernel, sum(v.shape[0] for v in parts), *parts)


def product_kernel(*refs):
    n_row, n_col = len(ROW_PARTS), len(COL_PARTS)
    row_refs, col_refs = refs[:n_row], refs[n_row : n_row + n_col]
    out_ref, rows, *tiles = refs[n_row + n_col :]
    row, my_y = lax.axis_index("row"), lax.axis_index("col") // ZH
    my_z, my_x, my_c = row // (XN * CN), lax.rem(row // CN, XN), lax.rem(row, CN)
    sign = 1 - 2 * my_c
    at_step = pl.program_id(0)
    block = 2 * WIDTH
    tall = block * YN
    wide = XN * CN * WIDTH

    def fill(to, z):
        mirrored = (z // TRIPLE != my_z // TRIPLE).astype(jnp.int32)
        near = z + mirrored * (ZL - 1 - 2 * z)
        ahead = lax.rem(lax.rem(near, TRIPLE) - lax.rem(my_z, TRIPLE) + TRIPLE, TRIPLE)
        frm = (2 * ahead + mirrored) * WIDTH
        for ref, parts in zip(col_refs, COL_PARTS):
            for at, (dx, s) in enumerate(parts):
                x = lax.rem(my_x + sign * dx + XN, XN)
                c = my_c + s - 2 * my_c * s
                put = pl.multiple_of((x * CN + c) * WIDTH, WIDTH)
                start = pl.multiple_of(at * ZL * WIDTH + frm, WIDTH)
                h, l = split(ref[pl.ds(start, WIDTH), :])
                to[0][pl.ds(put, WIDTH), :] = h
                to[1][pl.ds(put, WIDTH), :] = l

    def multiply(tile):
        both = dot_t(rows[...], tile[0][...])
        return both[:tall] + (both[tall:] + dot_t(rows[:tall], tile[1][...]))

    @pl.when(at_step == 0)
    def _():
        for ref, parts in zip(row_refs, ROW_PARTS):
            for at, dy in enumerate(parts):
                h, l = split(ref[at * block : (at + 1) * block, :])
                to = pl.multiple_of(lax.rem(my_y + sign * dy + YN, YN) * block, block)
                rows[pl.ds(to, block), :] = h
                rows[pl.ds(tall + to, block), :] = l
        fill(tiles[:2], 0 * at_step)

    out_ref[:, :wide] = multiply(tiles[:2])
    fill(tiles[2:], 2 * at_step + 1)
    out_ref[:, wide:] = multiply(tiles[2:])
    fill(tiles[:2], jnp.minimum(2 * at_step + 2, ZL - 1))


def product(rows, cols):
    whole = pl.BlockSpec(memory_space=pltpu.VMEM)
    tall, deep = 2 * WIDTH * YN, rows[0].shape[1]
    wide = XN * CN * WIDTH
    return pl.pallas_call(
        product_kernel,
        out_shape=jax.ShapeDtypeStruct((tall, ZL * wide), jnp.float32),
        grid=(ZL // 2,),
        in_specs=[whole] * (len(rows) + len(cols)),
        out_specs=pl.BlockSpec((tall, 2 * wide), lambda i: (0, i)),
        scratch_shapes=[pltpu.VMEM((2 * tall, deep), jnp.bfloat16)]
        + [pltpu.VMEM((wide, deep), jnp.bfloat16)] * 4,
        compiler_params=pltpu.CompilerParams(vmem_limit_bytes=28 * 2**20),
    )(*rows, *cols)


def step(harmonic, legendre, whitening, longitude, observed):
    own, rhs_part = whiten(harmonic, legendre, whitening, longitude, observed)

    swap = lambda z, x, c: (z, x, 1 - c)
    block, twin = scatter(own, 0), scatter(own, 1)
    mirror = from_row(own, lambda z, x, c: (ZL - 1 - z, x, c))
    pair = local(pair_kernel, 2 * WIDTH, block, twin)

    two = join(own, mirror)
    near = [from_row(two, lambda z, x, c, d=d: (in_triple(z, d), x, c)) for d in (1, 2)]
    line = join(two, *near)

    y4 = from_y(pair, 4, 4)
    quad = join(pair, y4)
    y2 = from_y(quad, 2, -2)
    y1 = from_y(join(quad, y2), 1, -1)

    ahead = lambda z, x, c: (z, (x + 1 - 2 * c) % XN, c)
    line_b = from_row(line, swap)
    x1, w1 = from_row(line, ahead), from_row(line_b, ahead)
    x2 = from_row(x1, ahead)
    back = [from_row(v, swap) for v in (x1, w1, x2)]
    return product([pair, y4, y2, y1], [line, line_b, x1, w1, x2] + back), rhs_part


def solution(mesh):
    in_specs = (P("col", "row"), P(None, "col", "row", None), P(), P(), P())
    out_specs = (P("row", "col"), P("col", "row"))
    return jax.shard_map(step, mesh=mesh, in_specs=in_specs, out_specs=out_specs, check_vma=False)
```

```python
import jax
import jax.numpy as jnp
from jax import lax
from jax.experimental import pallas as pl
from jax.experimental.pallas import tpu as pltpu
from jax.sharding import PartitionSpec as P


LMAX = 156
ZL, XN, CN, YN, ZH = 6, 4, 2, 8, 2
WIDTH = 32
TRIPLE = ZL // 2


def from_row(value, source):
    place = lambda z, x, c: (z * XN + x) * CN + c
    every = [(z, x, c) for z in range(ZL) for x in range(XN) for c in range(CN)]
    return lax.ppermute(value, "row", [(place(*source(*at)), place(*at)) for at in every])


def from_y(value, dy, other):
    rows, cols = ZL * XN * CN, YN * ZH
    pairs = [
        (r * cols + (y + (dy, other)[r % CN]) % YN * ZH + h, r * cols + y * ZH + h)
        for r in range(rows)
        for y in range(YN)
        for h in range(ZH)
    ]
    return lax.ppermute(value, ("row", "col"), pairs)


def scatter(value, flip):
    rows, cols = ZL * XN * CN, YN * ZH
    pairs = [
        (big_r * cols + big_c, (rows // cols * big_c + big_r // cols) * cols + (big_r % cols ^ flip))
        for big_r in range(rows)
        for big_c in range(cols)
    ]
    return lax.ppermute(value, ("row", "col"), pairs)


def in_triple(z, d):
    return z // TRIPLE * TRIPLE + (z % TRIPLE + d) % TRIPLE


def split(value):
    high = value.astype(jnp.bfloat16)
    low = (value - high.astype(jnp.float32)).astype(jnp.bfloat16)
    return high, low


def dot_t(a, b):
    return lax.dot_general(a, b, (((1,), (1,)), ((), ())), preferred_element_type=jnp.float32)


def to_column(value):
    n = value.shape[1]
    same = lax.broadcasted_iota(jnp.int32, (n, n), 0) == lax.broadcasted_iota(jnp.int32, (n, n), 1)
    return jnp.sum(jnp.where(same, jnp.broadcast_to(value, (n, n)), 0.0), axis=1, keepdims=True)


def to_row(value):
    n = value.shape[0]
    same = lax.broadcasted_iota(jnp.int32, (n, n), 0) == lax.broadcasted_iota(jnp.int32, (n, n), 1)
    return jnp.sum(jnp.where(same, jnp.broadcast_to(value, (n, n)), 0.0), axis=0, keepdims=True)


def trig(angle, is_cosine):
    turns = jnp.floor(angle * 0.6366197723675814 + 0.5)
    rest = angle - turns * 1.5703125
    rest = rest - turns * 4.837512969970703125e-4
    rest = rest - turns * 7.54978995489188216e-8
    quadrant = (turns.astype(jnp.int32) + jnp.where(is_cosine, 0, 3)) & 3
    sq = rest * rest
    sine = ((-1.9515295891e-4 * sq + 8.3321608736e-3) * sq - 1.6666654611e-1) * sq * rest + rest
    cosine = ((2.443315711809948e-5 * sq - 1.388731625493765e-3) * sq + 4.166664568298827e-2) * sq * sq
    cosine = cosine - 0.5 * sq + 1.0
    value = jnp.where((quadrant & 1) == 0, cosine, sine)
    return jnp.where((quadrant == 1) | (quadrant == 2), -value, value)


def whiten_kernel(*refs):
    sources, (own_ref, rhs_ref), buffers, sems = refs[:5], refs[5:7], refs[7:12], refs[12]
    harmonic, legendre, whitening, longitude, observed = buffers
    arcs = longitude.shape[0]
    copies = [pltpu.make_async_copy(sources[i], buffers[i], sems.at[i]) for i in (0, 3, 4, 1)]
    parts = [
        pltpu.make_async_copy(sources[2].at[a], whitening.at[a], sems.at[5 + a]) for a in range(arcs)
    ]
    for copy in copies + parts:
        copy.start()
    for copy in copies:
        copy.wait()
    azimuth = to_column(harmonic[...].astype(jnp.float32))
    is_cosine = azimuth <= float(LMAX)
    order = jnp.where(is_cosine, azimuth, azimuth - float(LMAX))
    total = None
    for arc in range(arcs):
        terms = trig(order * longitude[arc : arc + 1, :], is_cosine)
        design = legendre[arc, 0] * terms
        seen = jnp.broadcast_to(observed[arc : arc + 1, :], (8, observed.shape[1]))
        dh, dl = split(jnp.concatenate([design, seen], axis=0))
        parts[arc].wait()
        wh, wl = split(whitening[arc])
        n = dh.shape[0]
        both = dot_t(jnp.concatenate([dh, dl], axis=0), wh)
        out = both[:n] + both[n:] + dot_t(dh, wl)
        own = out[:WIDTH]
        own_ref[:, arc * own.shape[1] : (arc + 1) * own.shape[1]] = own
        part = jnp.sum(own * out[WIDTH : WIDTH + 1], axis=1, keepdims=True)
        total = part if total is None else total + part
    rhs_ref[...] = to_row(total)


def whiten(*args):
    arcs, obs = args[3].shape
    return pl.pallas_call(
        whiten_kernel,
        out_shape=(
            jax.ShapeDtypeStruct((WIDTH, arcs * obs), jnp.float32),
            jax.ShapeDtypeStruct((1, WIDTH), jnp.float32),
        ),
        in_specs=[pl.BlockSpec(memory_space=pl.ANY)] * len(args),
        out_specs=(pl.BlockSpec(memory_space=pltpu.VMEM),) * 2,
        scratch_shapes=[pltpu.VMEM(v.shape, v.dtype) for v in args]
        + [pltpu.SemaphoreType.DMA((5 + arcs,))],
        compiler_params=pltpu.CompilerParams(vmem_limit_bytes=16 * 2**20),
    )(*[pltpu.with_memory_space_constraint(v, pltpu.HBM) for v in args])


ROW_PARTS = ((0,), (4,), (2, 6), (1, 5), (3, 7))
COL_PARTS = (((0, 0),), ((0, 1),), ((1, 0),), ((1, 1),), ((2, 0),), ((-1, 1),), ((-1, 0),), ((2, 1),))


def join_kernel(*refs):
    at = 0
    for ref in refs[:-1]:
        refs[-1][at : at + ref.shape[0], :] = ref[...]
        at += ref.shape[0]


def pair_kernel(block, twin, out):
    n = block.shape[0]
    mine = lax.rem(lax.axis_index("col"), ZH)
    out[pl.ds(pl.multiple_of(mine * n, n), n), :] = block[...]
    out[pl.ds(pl.multiple_of((1 - mine) * n, n), n), :] = twin[...]


def local(kernel, length, *parts):
    on_core = pl.BlockSpec(memory_space=pltpu.VMEM)
    return pl.pallas_call(
        kernel,
        out_shape=jax.ShapeDtypeStruct((length, parts[0].shape[1]), parts[0].dtype),
        in_specs=[on_core] * len(parts),
        out_specs=on_core,
        compiler_params=pltpu.CompilerParams(vmem_limit_bytes=16 * 2**20),
    )(*parts)


def join(*parts):
    return local(join_kernel, sum(v.shape[0] for v in parts), *parts)


def product_kernel(*refs):
    n_row, n_col = len(ROW_PARTS), len(COL_PARTS)
    row_refs, col_refs = refs[:n_row], refs[n_row : n_row + n_col]
    out_ref, rows, *tiles = refs[n_row + n_col :]
    row, my_y = lax.axis_index("row"), lax.axis_index("col") // ZH
    my_z, my_x, my_c = row // (XN * CN), lax.rem(row // CN, XN), lax.rem(row, CN)
    sign = 1 - 2 * my_c
    at_step = pl.program_id(0)
    block = 2 * WIDTH
    tall = block * YN
    wide = XN * CN * WIDTH

    def fill(to, z):
        mirrored = (z // TRIPLE != my_z // TRIPLE).astype(jnp.int32)
        near = z + mirrored * (ZL - 1 - 2 * z)
        ahead = lax.rem(lax.rem(near, TRIPLE) - lax.rem(my_z, TRIPLE) + TRIPLE, TRIPLE)
        frm = (2 * ahead + mirrored) * WIDTH
        for ref, parts in zip(col_refs, COL_PARTS):
            for at, (dx, s) in enumerate(parts):
                x = lax.rem(my_x + sign * dx + XN, XN)
                c = my_c + s - 2 * my_c * s
                put = pl.multiple_of((x * CN + c) * WIDTH, WIDTH)
                start = pl.multiple_of(at * ZL * WIDTH + frm, WIDTH)
                h, l = split(ref[pl.ds(start, WIDTH), :])
                to[0][pl.ds(put, WIDTH), :] = h
                to[1][pl.ds(put, WIDTH), :] = l

    def multiply(tile):
        both = dot_t(rows[...], tile[0][...])
        return both[:tall] + (both[tall:] + dot_t(rows[:tall], tile[1][...]))

    @pl.when(at_step == 0)
    def _():
        for ref, parts in zip(row_refs, ROW_PARTS):
            for at, dy in enumerate(parts):
                h, l = split(ref[at * block : (at + 1) * block, :])
                to = pl.multiple_of(lax.rem(my_y + sign * dy + YN, YN) * block, block)
                rows[pl.ds(to, block), :] = h
                rows[pl.ds(tall + to, block), :] = l
        fill(tiles[:2], 0 * at_step)

    out_ref[:, :wide] = multiply(tiles[:2])
    fill(tiles[2:], 2 * at_step + 1)
    out_ref[:, wide:] = multiply(tiles[2:])
    fill(tiles[:2], jnp.minimum(2 * at_step + 2, ZL - 1))


def product(rows, cols):
    whole = pl.BlockSpec(memory_space=pltpu.VMEM)
    tall, deep = 2 * WIDTH * YN, rows[0].shape[1]
    wide = XN * CN * WIDTH
    return pl.pallas_call(
        product_kernel,
        out_shape=jax.ShapeDtypeStruct((tall, ZL * wide), jnp.float32),
        grid=(ZL // 2,),
        in_specs=[whole] * (len(rows) + len(cols)),
        out_specs=pl.BlockSpec((tall, 2 * wide), lambda i: (0, i)),
        scratch_shapes=[pltpu.VMEM((2 * tall, deep), jnp.bfloat16)]
        + [pltpu.VMEM((wide, deep), jnp.bfloat16)] * 4,
        compiler_params=pltpu.CompilerParams(vmem_limit_bytes=28 * 2**20),
    )(*rows, *cols)


def step(harmonic, legendre, whitening, longitude, observed):
    own, rhs_part = whiten(harmonic, legendre, whitening, longitude, observed)

    swap = lambda z, x, c: (z, x, 1 - c)
    block, twin = scatter(own, 0), scatter(own, 1)
    mirror = from_row(own, lambda z, x, c: (ZL - 1 - z, x, c))
    pair = local(pair_kernel, 2 * WIDTH, block, twin)

    two = join(own, mirror)
    near = [from_row(two, lambda z, x, c, d=d: (in_triple(z, d), x, c)) for d in (1, 2)]
    line = join(two, *near)

    y4 = from_y(pair, 4, 4)
    quad = join(pair, y4)
    y2 = from_y(quad, 2, -2)
    y5, y1 = from_y(quad, 1, -1), from_y(y2, 1, -1)

    ahead = lambda z, x, c: (z, (x + 1 - 2 * c) % XN, c)
    line_b = from_row(line, swap)
    x1, w1 = from_row(line, ahead), from_row(line_b, ahead)
    x2 = from_row(x1, ahead)
    back = [from_row(v, swap) for v in (x1, w1, x2)]
    return product([pair, y4, y2, y5, y1], [line, line_b, x1, w1, x2] + back), rhs_part


def solution(mesh):
    in_specs = (P("col", "row"), P(None, "col", "row", None), P(), P(), P())
    out_specs = (P("row", "col"), P("col", "row"))
    return jax.shard_map(step, mesh=mesh, in_specs=in_specs, out_specs=out_specs, check_vma=False)
```
